32 devices in a mesh: pages: 8 (over z, core), blocks: 4 (over y, x).
Axes of the slice: x: 2, y: 2, z: 4, core: 2. Of those that a mesh axis runs over, the one named last changes fastest.
Arguments:
- queries: bfloat16 [64, 24, 128], P(('pages', 'blocks')), may hold values from -0.5 to 0.5
- centroids: bfloat16 [256, 128], replicated, may hold values from -6 to 6
- basis: bfloat16 [256, 32, 128], replicated, may hold values from -1 to 1
- patch_ids: int32 [8, 32, 256], P('pages', None, 'blocks'), may hold values from 0 to 255
- coeffs: bfloat16 [8, 32, 8192], P('pages', None, 'blocks'), may hold values from -6 to 6
- page_counts: int32 [8, 32], P('pages'), may hold values from 128 to 256
- cand_ids: int32 [8, 64, 16], P('pages'), may hold values from 0 to 31
- cand_counts: int32 [8, 64], P('pages'), may hold values from 0 to 16, as said below
Outputs:
- scores: float32 [64, 8, 16], P(('pages', 'blocks'))
The draws below stay inside these ranges and needn't reach their ends.
Inputs may be any that keep to these rules, and one draw needn't show every extreme that they name: `cand_ids`: slots at or past a query's count in a group are padding and name arbitrary pages; ids may repeat. `cand_counts`: each query's counts over the 8 groups add up to 64.
All inputs are finite; a program needn't handle non-finite values.
Results may differ from the reference program's by a relative error of at most 0.00065.
Values may be sent and summed in bfloat16 or wider, within the bound.
A program may use at most 64 MiB of HBM per device.

```python
import jax
import jax.numpy as jnp
from jax import lax

DIM = 128
QTOK = 24
RANK = 32
NCENT = 256
CANDS = 64
PAGES_GRP = 32
NGROUPS = 8
NQ = 64
CMAX = 16
PATCHES = 256


def draw_page_counts(key, part):
    counts = jax.random.randint(key, (NGROUPS, PAGES_GRP), PATCHES // 2, PATCHES + 1)
    return counts.at[0, 0].set(PATCHES)


def draw_cand_counts(key, part):
    even_share = CANDS // NGROUPS
    key_heat, key_pair, key_move = jax.random.split(key, 3)
    heat_rank = jax.random.permutation(key_heat, NGROUPS)
    pairing = jax.vmap(lambda subkey: jax.random.permutation(subkey, NGROUPS))(jax.random.split(key_pair, NQ))
    pair_left = pairing[:, 0::2]
    pair_right = pairing[:, 1::2]
    moved_count = even_share - jax.random.randint(key_move, (NQ, NGROUPS // 2), 0, even_share // 4 + 1)
    moved_count = moved_count.at[0, 0].set(even_share)
    left_hot = heat_rank[pair_left] > heat_rank[pair_right]
    winner_group = jnp.where(left_hot, pair_left, pair_right)
    loser_group = jnp.where(left_hot, pair_right, pair_left)
    row_index = jnp.arange(NQ)[:, None]
    counts = jnp.zeros((NQ, NGROUPS), jnp.int32)
    counts = counts.at[row_index, winner_group].set(even_share + moved_count)
    counts = counts.at[row_index, loser_group].set(even_share - moved_count)
    return counts.T


def touch_ends(values, rng, low, high):
    spot = [jax.random.randint(jax.random.fold_in(rng, axis), (), 0, length) for axis, length in enumerate(values.shape)]
    widest = values.shape.index(max(values.shape))
    next_to = spot[:widest] + [(spot[widest] + 1) % values.shape[widest]] + spot[widest + 1:]
    return values.at[tuple(spot)].set(low).at[tuple(next_to)].set(high)


def level_of(key, shape, cuts, smallest, top_value):
    loudness, own = 1.0, jax.random.fold_in(key, 6)
    for dim, parts in cuts:
        steps = jnp.exp(jax.random.uniform(jax.random.fold_in(own, dim), (parts,), jnp.float32, smallest / len(cuts), top_value / len(cuts)))
        loudness = loudness * jnp.repeat(steps, shape[dim] // parts).reshape([-1 if axis == dim else 1 for axis in range(len(shape))])
    return loudness


def centred(key, extent, deviation, reach, shards=(), held_as=jnp.bfloat16):
    drawn = jax.random.normal(key, extent, jnp.float32) * deviation
    if len(shards) > 0:
        drawn = level_of(key, extent, shards, -0.22, 0.18) * drawn
    return jnp.clip(drawn, min=-reach, max=reach).astype(held_as)


def setup_inputs(seed: int = 0) -> dict:
    splits = jax.random.split(jax.random.key(seed), 9)
    return {
        "queries": centred(splits[0], (NQ, QTOK, DIM), DIM ** -0.5, 0.5, ((0, 32),)),
        "centroids": centred(splits[1], (NCENT, DIM), 1.0, 6.0),
        "basis": centred(splits[2], (NCENT, RANK, DIM), RANK ** -0.5, 1.0),
        "patch_ids": touch_ends(jax.random.randint(splits[3], (NGROUPS, PAGES_GRP, PATCHES), 0, NCENT), jax.random.fold_in(splits[3], 1), 0, NCENT - 1).astype(jnp.int32),
        "coeffs": centred(splits[4], (NGROUPS, PAGES_GRP, PATCHES * RANK), 1.0, 6.0, ((0, 8), (2, 4))),
        "page_counts": draw_page_counts(jax.random.fold_in(splits[8], 71), 0),
        "cand_ids": touch_ends(jax.random.randint(splits[6], (NGROUPS, NQ, CMAX), 0, PAGES_GRP), jax.random.fold_in(splits[6], 1), 0, PAGES_GRP - 1).astype(jnp.int32),
        "cand_counts": draw_cand_counts(jax.random.fold_in(splits[8], 71), 0),
    }


def decode_group(group_ids, group_coef, centroids, basis):
    def one_page(inputs):
        page_ids, page_coef = inputs
        center = centroids[page_ids].astype(jnp.float32)
        chosen = basis[page_ids].astype(jnp.float32)
        coeff_rows = page_coef.reshape(PATCHES, RANK).astype(jnp.float32)
        residual = jnp.einsum("nj,njd->nd", coeff_rows, chosen)
        return (center + residual).astype(jnp.bfloat16)
    return lax.map(one_page, (group_ids, group_coef))


def score_group(group_emb, group_live, group_cands, group_counts, queries):
    patch_pos = jnp.arange(PATCHES, dtype=jnp.int32)
    slot_pos = jnp.arange(CMAX, dtype=jnp.int32)

    def one_block(inputs):
        query_group, cand_group, count_group = inputs
        chosen = group_emb[cand_group].astype(jnp.float32)
        similar = jnp.einsum("gcpd,gtd->gcpt", chosen, query_group.astype(jnp.float32))
        valid_patch = patch_pos[None, None, :] < group_live[cand_group][:, :, None]
        similar = jnp.where(valid_patch[..., None], similar, -jnp.inf)
        block_best = jnp.max(similar, axis=2)
        slot_used = slot_pos[None, :] < count_group[:, None]
        return jnp.where(slot_used[..., None], block_best, 0.0).astype(jnp.bfloat16)

    blocks = NQ // 16
    results = lax.map(one_block, (queries.reshape(blocks, 16, QTOK, DIM), group_cands.reshape(blocks, 16, CMAX), group_counts.reshape(blocks, 16)))
    return results.reshape(NQ, CMAX, QTOK)


def reference(queries, centroids, basis, patch_ids, coeffs, page_counts, cand_ids, cand_counts):
    def per_group(inputs):
        group_ids, group_coef, group_live, group_cands, group_counts = inputs
        group_emb = decode_group(group_ids, group_coef, centroids, basis)
        return score_group(group_emb, group_live, group_cands, group_counts, queries)

    block_best = lax.map(per_group, (patch_ids, coeffs, page_counts, cand_ids, cand_counts))
    scores = jnp.sum(block_best.astype(jnp.float32), axis=3) / QTOK
    return jnp.transpose(scores, (1, 0, 2))
```

```python
import functools

import jax
import jax.numpy as jnp
from jax import lax
from jax.experimental import pallas as pl
from jax.experimental.pallas import tpu as pltpu
from jax.sharding import PartitionSpec as P

MESH = pl.DeviceIdType.MESH
SPLIT = 4
STEP = 8
AHEAD, NEAR, FAR = 1, 3, 4
LOWEST = -3.0e38


def remote(src, dst, send, recv, where):
    return pltpu.make_async_remote_copy(
        src_ref=src, dst_ref=dst, send_sem=send, recv_sem=recv, device_id=where, device_id_type=MESH
    )


def flip(index, bits):
    for bit in range(bits.bit_length()):
        if bits >> bit & 1:
            index = index + 2**bit - 2 ** (bit + 1) * lax.rem(lax.div(index, 2**bit), 2)
    return index


def far_first(count):
    return sorted(range(1, count), key=lambda s: -s.bit_count())


def kernel(
    n_pages, n_blocks, qtok,
    q_hbm, cent_hbm, basis_hbm, ids_hbm, coef_hbm, count_hbm, cand_hbm, live_hbm, out_ref,
    cent, basis, ids, coef, count, cand, live,
    qbuf, idb, dlow, emb, first, bound, outgo, income, gather, scoreT, piece, landed,
    in_sem, z_send, z_recv, b_send, b_recv, c_send, c_recv, d_send, d_recv, e_send, e_recv,
):
    k = lax.axis_index("pages")
    r = lax.axis_index("blocks")
    core = lax.rem(k, 2)
    z = lax.div(k, 2)
    nz = n_pages // 2
    pages, patches = ids.shape
    cents, width = cent.shape
    rank = basis.shape[0] // cents
    rows_q = q_hbm.shape[0]
    cols = n_pages * rows_q

    barrier = pltpu.get_barrier_semaphore()
    for s in range(1, n_pages):
        pl.semaphore_signal(
            barrier, inc=1, device_id=(lax.rem(k + s, n_pages), r), device_id_type=MESH
        )
    for s in range(1, n_blocks):
        pl.semaphore_signal(
            barrier, inc=1, device_id=(k, lax.rem(r + s, n_blocks)), device_id_type=MESH
        )

    own = qbuf.at[r, core, pl.ds(pl.multiple_of(z * rows_q, rows_q), rows_q), :]
    loads = [
        pltpu.make_async_copy(src, dst, in_sem.at[i])
        for i, (src, dst) in enumerate(
            [
                (ids_hbm, ids), (count_hbm, count), (q_hbm, own), (coef_hbm, coef),
                (cent_hbm, cent), (basis_hbm, basis), (cand_hbm, cand), (live_hbm, live),
            ]
        )
    ]
    for copy in loads:
        copy.start()

    loads[0].wait()
    loads[1].wait()
    low_total = cents // SPLIT
    lane_cent = lax.div(lax.broadcasted_iota(jnp.int32, (1, STEP * width), 1), rank)
    lane_cent = lax.rem(lane_cent, width // rank).astype(jnp.float32)
    id_f = ids[...].astype(jnp.float32)
    id_low = lax.bitwise_and(ids[...], low_total - 1).astype(jnp.float32)
    id_both = jnp.concatenate([id_f, id_low], axis=0).astype(jnp.bfloat16)
    to_col = lax.div(lax.broadcasted_iota(jnp.int32, (1, STEP * width), 1), width)
    from_row = lax.broadcasted_iota(jnp.int32, (STEP, STEP * width), 0)
    pick = (from_row == to_col).astype(jnp.float32).astype(jnp.bfloat16)
    for m in range(patches // STEP):
        wide = jnp.dot(
            id_both[:, m * STEP : (m + 1) * STEP], pick, preferred_element_type=jnp.float32
        )
        wide_id = wide[:pages].astype(jnp.bfloat16)
        wide_low = (wide[pages:] - lane_cent).astype(jnp.bfloat16)
        for p in range(STEP):
            idb[m * STEP + p] = wide_id[:, p * width : (p + 1) * width]
            dlow[m * STEP + p] = wide_low[:, p * width : (p + 1) * width]
    spread = jnp.broadcast_to(count[...].astype(jnp.float32), (pages, pages))
    diag = lax.broadcasted_iota(jnp.int32, (pages, pages), 0) == lax.broadcasted_iota(
        jnp.int32, (pages, pages), 1
    )
    column = jnp.sum(jnp.where(diag, spread, 0.0), axis=1, keepdims=True)
    bound[...] = jnp.broadcast_to(column, (pages, width)) - (r * patches).astype(jnp.float32)

    for copy in loads[3:]:
        copy.wait()

    n_query = cand.shape[1]
    per_dev = rows_q // qtok
    spot = lax.broadcasted_iota(jnp.int32, (1, cols), 1)
    seen = lax.broadcasted_iota(jnp.int32, (n_query, cols), 0)
    shard = lax.div(spot, rows_q)
    owner = lax.rem(shard, nz) * 2 + lax.div(shard, nz)
    index = (owner * n_blocks + r) * per_dev + lax.div(lax.rem(spot, rows_q), qtok)
    gather[...] = (index == seen).astype(jnp.float32).astype(jnp.bfloat16)

    per = width // rank
    tile_row = lax.broadcasted_iota(jnp.int32, (width, per * width), 0)
    tile_col = lax.broadcasted_iota(jnp.int32, (1, per * width), 1)
    tile = (
        (tile_row == lax.div(tile_col, width) * rank + lax.rem(tile_col, rank))
        .astype(jnp.float32)
        .astype(jnp.bfloat16)
    )
    depth = low_total * rank
    rows = STEP * pages

    def decode(m):
        base = m * STEP
        parts = []
        for h in range(STEP // per):
            chunk = coef[:, pl.ds(pl.multiple_of((m * (STEP // per) + h) * width, width), width)]
            spreadc = jnp.dot(chunk, tile, preferred_element_type=jnp.float32)
            for s in range(per):
                parts.append(spreadc[:, s * width : (s + 1) * width].astype(jnp.bfloat16))
        weights = jnp.concatenate(parts, axis=0)
        low = dlow[pl.ds(base, STEP)].reshape(rows, width)
        mine = idb[pl.ds(base, STEP)].reshape(rows, width)
        zero = jnp.zeros((rows, width), jnp.bfloat16)
        lhs = jnp.concatenate(
            [
                jnp.where(low == jnp.bfloat16(per * t), weights, zero)
                for t in range(depth // width)
            ],
            axis=1,
        )
        rhs = jnp.concatenate(
            [basis[h * depth : (h + 1) * depth, :] for h in range(SPLIT)], axis=1
        )
        res = jnp.dot(lhs, rhs, preferred_element_type=jnp.float32)
        lane_id = lax.broadcasted_iota(jnp.int32, (rows, width), 1).astype(jnp.float32).astype(jnp.bfloat16)
        one = jnp.ones((rows, width), jnp.bfloat16)
        hot = jnp.concatenate(
            [
                jnp.where(mine == lane_id + jnp.bfloat16(t * width), one, zero)
                for t in range(cents // width)
            ],
            axis=1,
        )
        center = jnp.dot(hot, cent[...], preferred_element_type=jnp.float32)
        mine_f = mine.astype(jnp.float32)
        total = res[:, :width]
        for h in range(1, SPLIT):
            total = jnp.where(
                mine_f >= float(h * low_total), res[:, h * width : (h + 1) * width], total
            )
        total = (total + center).reshape(STEP, pages, width)

        @pl.when(m == 0)
        def _():
            first[...] = total[0]

        position = base + lax.broadcasted_iota(jnp.int32, (STEP, pages, width), 0)
        valid = position.astype(jnp.float32) < bound[...][None]
        total = jnp.where(valid, total, first[...][None])
        emb[pl.ds(pl.multiple_of(m * rows, rows), rows), :] = total.astype(jnp.bfloat16).reshape(rows, width)

    turns = patches // STEP

    def decode_steps(start, stop):
        start, stop = min(start, turns), min(stop, turns)
        if stop > start:
            lax.fori_loop(start, stop, lambda m, carry: (decode(m), carry)[1], 0)

    def shard_at(block, where):
        return qbuf.at[block, core, pl.ds(pl.multiple_of(where * rows_q, rows_q), rows_q), :]

    decode_steps(0, AHEAD)
    loads[2].wait()
    pl.semaphore_wait(barrier, n_pages - 1 + n_blocks - 1)
    z_copies = {
        s: remote(own, own, z_send.at[s], z_recv.at[s], (flip(z, s) * 2 + core, r))
        for s in far_first(nz)
    }
    for copy in z_copies.values():
        copy.start()
    b_copies = {}

    def forward(t):
        if t:
            z_copies[t].wait_recv()
        part = shard_at(r, flip(z, t))
        for s in far_first(n_blocks):
            b_copies[s, t] = remote(
                part, part, b_send.at[s, t], b_recv.at[s, t], (k, flip(r, s))
            )
            b_copies[s, t].start()

    forward(0)
    decode_steps(AHEAD, NEAR)
    for t in range(1, nz // 2 + 1):
        forward(t)
    decode_steps(NEAR, FAR)
    for t in range(nz // 2 + 1, nz):
        forward(t)
    partner = (k + 1 - 2 * core, r)

    def share(s):
        for t in range(nz):
            if s:
                b_copies[s, t].wait_recv()
        half = qbuf.at[flip(r, s), core]
        copy = remote(half, half, c_send.at[s], c_recv.at[s], partner)
        copy.start()
        return copy

    c_copies = {0: share(0)}
    decode_steps(FAR, turns)

    def best_of(source):
        query = qbuf[source].reshape(cols, width)

        best = jnp.full((pages, cols), LOWEST, jnp.float32)
        for m in range(turns):
            sim = lax.dot_general(
                emb[m * rows : (m + 1) * rows, :], query, (((1,), (1,)), ((), ())),
                preferred_element_type=jnp.float32,
            )
            best = jnp.maximum(best, jnp.max(sim.reshape(STEP, pages, cols), axis=0))
        return jnp.where(bound[:, :1] > 0.0, best, LOWEST).astype(jnp.bfloat16)

    c_copies[0].wait_recv()
    income[0] = best_of(r)
    for s in far_first(n_blocks):
        c_copies[s] = share(s)
    d_copies = []
    for s in far_first(n_blocks):
        c_copies[s].wait_recv()
        source = flip(r, s)
        outgo[s] = best_of(source)
        copy = remote(outgo.at[s], income.at[s], d_send.at[s], d_recv.at[s], (k, source))
        copy.start()
        d_copies.append(copy)

    slots = cand.shape[0]
    used = lax.broadcasted_iota(jnp.int32, (slots, n_query), 0) < live[...]
    chosen = cand[...]

    highest = income[0].astype(jnp.float32)
    for copy in d_copies:
        copy.wait_recv()
    for s in range(1, n_blocks):
        highest = jnp.maximum(highest, income[s].astype(jnp.float32))
    sums = lax.dot_general(
        highest.astype(jnp.bfloat16), gather[...], (((1,), (1,)), ((), ())),
        preferred_element_type=jnp.float32,
    )
    picked = jnp.zeros((slots, n_query), jnp.float32)
    for n in range(pages):
        picked = jnp.where(chosen == n, sums[n : n + 1, :], picked)
    picked = jnp.where(used, picked, 0.0)
    wide_q = scoreT.shape[0]
    padded = picked
    if wide_q > n_query:
        padded = jnp.concatenate([padded, jnp.zeros((slots, wide_q - n_query), jnp.float32)], axis=1)
    full = jnp.concatenate([padded, jnp.zeros((width - slots, wide_q), jnp.float32)], axis=0)
    scoreT[...] = full.T

    e_copies = []
    for s in range(n_pages - 1, -1, -1):
        to = flip(k, s)
        values = scoreT[pl.ds((to * n_blocks + r) * per_dev, per_dev), :]
        if s == 0:
            landed[k] = values
        else:
            piece[s] = values
            copy = remote(piece.at[s], landed.at[k], e_send.at[s], e_recv.at[s], (to, r))
            copy.start()
            e_copies.append(copy)
    for copy in e_copies:
        copy.wait_recv()
    for g in range(n_pages):
        arrived = landed[g]
        for i in range(per_dev):
            out_ref[i, g : g + 1, :] = arrived[i : i + 1, :slots]
    started = [*z_copies.values(), *b_copies.values(), *c_copies.values(), *d_copies, *e_copies]
    for copy in started:
        copy.wait_send()


def on_device(queries, centroids, basis, patch_ids, coeffs, page_counts, cand_ids, cand_counts):
    n_pages = lax.axis_size("pages")
    n_blocks = lax.axis_size("blocks")
    owned, qtok, width = queries.shape
    cents, rank, _ = basis.shape
    _, pages, patches = patch_ids.shape
    _, n_query, slots = cand_ids.shape
    rows_q = owned * qtok
    cols = n_pages * rows_q
    args = (
        queries.reshape(rows_q, width),
        centroids,
        basis.reshape(cents * rank, width),
        patch_ids[0],
        coeffs[0],
        page_counts,
        jnp.swapaxes(cand_ids[0], 0, 1),
        cand_counts,
    )
    dma = pltpu.SemaphoreType.DMA
    bf16, f32 = jnp.bfloat16, jnp.float32
    vmem = pltpu.VMEM
    totals = pl.pallas_call(
        functools.partial(kernel, n_pages, n_blocks, qtok),
        out_shape=vmem((owned, n_pages, slots), f32),
        in_specs=[pl.BlockSpec(memory_space=pl.ANY)] * len(args),
        out_specs=pl.BlockSpec(memory_space=pltpu.VMEM),
        scratch_shapes=[vmem(a.shape, a.dtype) for a in args[1:]]
        + [
            vmem((n_blocks, 2, cols // 2, width), bf16),
            vmem((patches, pages, width), bf16),
            vmem((patches, pages, width), bf16),
            vmem((patches * pages, width), bf16),
            vmem((pages, width), f32),
            vmem((pages, width), f32),
            vmem((n_blocks, pages, cols), bf16),
            vmem((n_blocks, pages, cols), bf16),
            vmem((n_query, cols), bf16),
            vmem((-(-n_query // 128) * 128, width), f32),
            vmem((n_pages, owned, width), f32),
            vmem((n_pages, owned, width), f32),
            dma((len(args),)),
            dma((n_pages,)), dma((n_pages,)),
            dma((n_blocks, n_pages // 2)), dma((n_blocks, n_pages // 2)),
            dma((n_blocks,)), dma((n_blocks,)),
            dma((n_blocks,)), dma((n_blocks,)),
            dma((n_pages,)), dma((n_pages,)),
        ],
        compiler_params=pltpu.CompilerParams(collective_id=0, has_side_effects=True),
    )(*args)
    return totals / qtok


def solution(mesh):
    placed = (
        P(("pages", "blocks"), None, None),
        P(),
        P(),
        P("pages", None, "blocks"),
        P("pages", None, "blocks"),
        P("pages", None),
        P("pages", None, None),
        P("pages", None),
    )
    return jax.shard_map(
        on_device,
        mesh=mesh,
        in_specs=placed,
        out_specs=P(("pages", "blocks"), None, None),
        check_vma=False,
    )
```

```python
import functools

import jax
import jax.numpy as jnp
from jax import lax
from jax.experimental import pallas as pl
from jax.experimental.pallas import tpu as pltpu
from jax.sharding import PartitionSpec as P

MESH = pl.DeviceIdType.MESH
DEPTH = 256
GROUP = 384
STEP = 8
LOWEST = -3.0e38


def remote(src, dst, send, recv, where):
    return pltpu.make_async_remote_copy(
        src_ref=src, dst_ref=dst, send_sem=send, recv_sem=recv, device_id=where, device_id_type=MESH
    )


def arrived(ref, sem):
    pltpu.make_async_copy(ref, ref, sem).wait()


def flip(index, bits):
    for bit in range(bits.bit_length()):
        if bits >> bit & 1:
            index = index + 2**bit - 2 ** (bit + 1) * lax.rem(lax.div(index, 2**bit), 2)
    return index


def to_bf16(mask):
    return mask.astype(jnp.float32).astype(jnp.bfloat16)


def kernel(
    n_pages, n_blocks, qtok,
    q_hbm, cent_hbm, basis_hbm, ids_hbm, coef_hbm, count_hbm, cand_hbm, live_hbm, out_ref,
    cent, basis, ids, spots, coef, count, cand, live,
    qbuf, raw, emb, first, bound, outgo, income, scoreT, piece, landed,
    in_sem, q_send, q_recv, x_send, x_recv, aux_send, aux_recv, d_send, d_recv, e_send, e_recv,
):
    k = lax.axis_index("pages")
    r = lax.axis_index("blocks")
    core = lax.rem(k, 2)
    z = lax.div(k, 2)
    nz = n_pages // 2
    hz = nz // 2
    pages, patches = ids.shape
    cents, rank, width = basis.shape
    rows_q = q_hbm.shape[0]
    per_dev = rows_q // qtok
    per = DEPTH // rank
    slots, n_query = cand_hbm.shape
    half_rows = n_blocks * hz * rows_q
    block_rows = hz * rows_q

    own_row = (r * hz + lax.rem(z, hz)) * rows_q
    own = qbuf.at[pl.ds(pl.multiple_of(own_row, rows_q), rows_q), :]
    loads = [
        pltpu.make_async_copy(src, dst, in_sem.at[i])
        for i, (src, dst) in enumerate(
            [
                (q_hbm, own), (ids_hbm, spots), (ids_hbm, ids), (count_hbm, count.at[0]),
                (coef_hbm, coef), (cent_hbm, cent), (basis_hbm, basis),
                (cand_hbm, cand.at[0]), (live_hbm, live.at[0]),
            ]
        )
    ]
    for copy in loads:
        copy.start()

    barrier = pltpu.get_barrier_semaphore()
    peers = [(t, s) for t in range(nz) for s in range(n_blocks) if t or s]
    peers.sort(key=lambda ts: (-(ts[0] >= hz), -(ts[0].bit_count() + ts[1].bit_count())))
    places = {ts: (flip(z, ts[0]) * 2 + core, flip(r, ts[1])) for ts in peers}
    partner = (k + 1 - 2 * core, r)
    for where in [*places.values(), partner]:
        pl.semaphore_signal(barrier, inc=1, device_id=where, device_id_type=MESH)
    loads[0].wait()
    pl.semaphore_wait(barrier, len(peers) + 1)
    q_copies = []
    for ts in peers:
        start = own_row + (half_rows if ts[0] >= hz else 0)
        land = qbuf.at[pl.ds(pl.multiple_of(start, rows_q), rows_q), :]
        copy = remote(own, land, q_send, q_recv.at[int(ts[0] >= hz)], places[ts])
        copy.start()
        q_copies.append(copy)
    aux_copies = [
        remote(src, dst.at[1], aux_send.at[i], aux_recv.at[i], partner)
        for i, (src, dst) in enumerate([(count_hbm, count), (cand_hbm, cand), (live_hbm, live)])
    ]
    for copy in aux_copies:
        copy.start()

    for copy in loads[1:7]:
        copy.wait()

    diag = lax.broadcasted_iota(jnp.int32, (pages, pages), 0) == lax.broadcasted_iota(
        jnp.int32, (pages, pages), 1
    )

    def set_bound(a):
        spread = jnp.broadcast_to(count[a].astype(jnp.float32), (pages, pages))
        column = jnp.sum(jnp.where(diag, spread, 0.0), axis=1, keepdims=True)
        bound[a] = jnp.broadcast_to(column, (pages, width)) - (r * patches).astype(jnp.float32)

    set_bound(0)
    rows16 = 2 * per
    mix = lax.broadcasted_iota(jnp.int32, (rows16, DEPTH), 1)
    turn = lax.rem(lax.div(mix, rank) + per - lax.rem(lax.broadcasted_iota(jnp.int32, (rows16, DEPTH), 0), per), per)
    turn = turn.astype(jnp.float32).astype(jnp.bfloat16)
    page_low = lax.rem(lax.broadcasted_iota(jnp.int32, (pages, width), 0), per)
    id_lane = lax.broadcasted_iota(jnp.int32, (pages, patches), 1)
    id_low = lax.rem(lax.broadcasted_iota(jnp.int32, (pages, patches), 0), per)
    lane_id = lax.broadcasted_iota(jnp.int32, (pages, width), 1).astype(jnp.float32).astype(jnp.bfloat16)
    one = jnp.ones((pages, width), jnp.bfloat16)
    zero = jnp.zeros((pages, width), jnp.bfloat16)
    chunk_rows = per * pages
    turns = patches // per

    def emb_chunk(slot, c):
        return emb.at[slot, pl.ds(pl.multiple_of(c * chunk_rows, chunk_rows), chunk_rows), :]

    def swap(c):
        return remote(emb_chunk(0, c), emb_chunk(1, c), x_send, x_recv, partner)

    def decode(c, carry):
        id_f = ids[...].astype(jnp.float32)
        hots = []
        for s in range(per):
            target = c * per + lax.rem(id_low + s, per)
            mine = jnp.sum(jnp.where(id_lane == target, id_f, 0.0), axis=1, keepdims=True)
            mine = jnp.broadcast_to(mine, (pages, width)).astype(jnp.bfloat16)
            hots.append(
                jnp.concatenate(
                    [
                        jnp.where(mine == lane_id + jnp.bfloat16(t * width), one, zero)
                        for t in range(cents // width)
                    ],
                    axis=1,
                )
            )
        center = jnp.dot(jnp.concatenate(hots, axis=0), cent[...], preferred_element_type=jnp.float32)
        raw[...] = center.reshape(per, pages, width)
        for h in range(pages // rows16):
            top = h * rows16
            weights = coef[top : top + rows16, pl.ds(pl.multiple_of(c * DEPTH, DEPTH), DEPTH)]
            for s in range(per):
                lhs = jnp.where(turn == jnp.bfloat16(s), weights, jnp.zeros_like(weights))
                sides = []
                for g in range(2):
                    chosen = [
                        basis[spots[top + g * per + (b - s) % per, c * per + b]] for b in range(per)
                    ]
                    sides.append(jnp.concatenate(chosen, axis=0))
                rhs = jnp.concatenate(sides, axis=1)
                res = jnp.dot(lhs, rhs, preferred_element_type=jnp.float32)
                both = jnp.concatenate([res[:per, :width], res[per:, width:]], axis=0)
                raw[s, top : top + rows16, :] = raw[s, top : top + rows16, :] + both

        @pl.when(c == 0)
        def _():
            start = raw[0]
            for s in range(1, per):
                start = jnp.where(page_low == per - s, raw[s], start)
            first[...] = start

        for s in range(per):
            position = (c * per + lax.rem(page_low + s, per)).astype(jnp.float32)
            total = jnp.where(position < bound[0], raw[s], first[...])
            emb[0, pl.ds(pl.multiple_of(c * chunk_rows + s * pages, pages), pages), :] = total.astype(jnp.bfloat16)

        @pl.when(c > 0)
        def _():
            swap(c - 1).start()

        return carry

    lax.fori_loop(0, turns, decode, 0)
    pad = -(-block_rows // 128) * 128
    aux_copies[0].wait_recv()
    set_bound(1)
    swap(turns - 1).start()

    spot = lax.broadcasted_iota(jnp.int32, (1, pad), 1)
    seen = lax.broadcasted_iota(jnp.int32, (n_query, pad), 0)

    def gather(h):
        away = flip(z, h * hz)
        z_abs = lax.div(away, hz) * hz + lax.div(spot, rows_q)
        index = ((z_abs * 2 + core) * n_blocks + r) * per_dev + lax.div(lax.rem(spot, rows_q), qtok)
        index = jnp.where(spot < block_rows, index, -1)
        return to_bf16(index == seen)

    blocks_at_once = min(n_blocks, max(1, GROUP // block_rows))
    cols = blocks_at_once * block_rows
    rows = STEP * pages

    def score(h, a):
        for b in range(0, n_blocks, blocks_at_once):
            begin = h * half_rows + b * block_rows
            query = qbuf[begin : begin + cols, :]
            best = jnp.full((pages, cols), LOWEST, jnp.float32)
            for m in range(patches // STEP):
                sim = lax.dot_general(
                    emb[a, m * rows : (m + 1) * rows, :], query, (((1,), (1,)), ((), ())),
                    preferred_element_type=jnp.float32,
                )
                best = jnp.maximum(best, jnp.max(sim.reshape(STEP, pages, cols), axis=0))
            best = jnp.where(bound[a][:, :1] > 0.0, best, LOWEST)
            for i in range(blocks_at_once):
                part = best[:, i * block_rows : (i + 1) * block_rows]
                if pad > block_rows:
                    part = jnp.concatenate([part, jnp.zeros((pages, pad - block_rows), jnp.float32)], axis=1)
                outgo[h * n_blocks + b + i, a * pages : (a + 1) * pages, :] = part.astype(jnp.bfloat16)

    d_copies = []

    def reduce_start(h):
        for s in sorted(range(1, n_blocks), key=lambda s: -s.bit_count()):
            copy = remote(
                outgo.at[h * n_blocks + flip(r, s)], income.at[h * n_blocks + s],
                d_send, d_recv.at[h], (k, flip(r, s)),
            )
            copy.start()
            d_copies.append(copy)

    def reduce_end(h):
        arrived(income.at[h * n_blocks + 1 : (h + 1) * n_blocks], d_recv.at[h])
        highest = outgo[h * n_blocks + r].astype(jnp.float32)
        for s in range(1, n_blocks):
            highest = jnp.maximum(highest, income[h * n_blocks + s].astype(jnp.float32))
        return lax.dot_general(
            highest.astype(jnp.bfloat16), gather(h), (((1,), (1,)), ((), ())),
            preferred_element_type=jnp.float32,
        )

    arrived(qbuf.at[0 : half_rows - rows_q], q_recv.at[0])
    score(0, 0)
    arrived(emb.at[1], x_recv)
    score(0, 1)
    reduce_start(0)
    for copy in [*loads[7:]]:
        copy.wait()
    for copy in aux_copies[1:]:
        copy.wait_recv()
    arrived(qbuf.at[half_rows : 2 * half_rows], q_recv.at[1])
    score(1, 0)
    score(1, 1)
    reduce_start(1)
    sums = reduce_end(0)
    sums = sums + reduce_end(1)

    slot = lax.broadcasted_iota(jnp.int32, (slots, n_query), 0)
    picks = []
    for a in range(2):
        chosen = cand[a]
        picked = jnp.zeros((slots, n_query), jnp.float32)
        for n in range(pages):
            picked = jnp.where(chosen == n, sums[a * pages + n : a * pages + n + 1, :], picked)
        picks.append(jnp.where(slot < live[a], picked, 0.0))
    even = core == 0
    wide_q = scoreT.shape[0]
    stacked = []
    for low, high in (picks, picks[::-1]):
        tall = jnp.where(even, low, high)
        stacked += [tall, jnp.zeros((width // 2 - slots, n_query), jnp.float32)]
    full = jnp.concatenate(stacked, axis=0)
    if wide_q > n_query:
        full = jnp.concatenate([full, jnp.zeros((width, wide_q - n_query), jnp.float32)], axis=1)
    scoreT[...] = full.T

    e_copies = []
    for t in range(nz - 1, -1, -1):
        to = flip(z, t)
        values = scoreT[pl.ds(((to * 2 + core) * n_blocks + r) * per_dev, per_dev), :]
        if t == 0:
            landed[z] = values
        else:
            piece[t] = values
            copy = remote(piece.at[t], landed.at[z], e_send, e_recv, (to * 2 + core, r))
            copy.start()
            e_copies.append(copy)
    total_q = len(peers) * rows_q
    arrived(qbuf.at[0:total_q], q_send)
    arrived(emb.at[0], x_send)
    arrived(income.at[0 : len(d_copies)], d_send)
    for copy in aux_copies:
        copy.wait_send()
    arrived(landed.at[1:nz], e_recv)
    for zs in range(nz):
        values = landed[zs]
        for p in range(2):
            for i in range(per_dev):
                out_ref[i, 2 * zs + p : 2 * zs + p + 1, :] = values[
                    i : i + 1, p * (width // 2) : p * (width // 2) + slots
                ]
    arrived(piece.at[1:nz], e_send)


def on_device(queries, centroids, basis, patch_ids, coeffs, page_counts, cand_ids, cand_counts):
    n_pages = lax.axis_size("pages")
    n_blocks = lax.axis_size("blocks")
    owned, qtok, width = queries.shape
    cents, rank, _ = basis.shape
    _, pages, patches = patch_ids.shape
    _, n_query, slots = cand_ids.shape
    rows_q = owned * qtok
    nz = n_pages // 2
    block_rows = nz // 2 * rows_q
    pad = -(-block_rows // 128) * 128
    args = (
        queries.reshape(rows_q, width),
        centroids,
        basis,
        patch_ids[0],
        coeffs[0],
        page_counts,
        jnp.swapaxes(cand_ids[0], 0, 1),
        cand_counts,
    )
    dma = pltpu.SemaphoreType.DMA
    bf16, f32, i32 = jnp.bfloat16, jnp.float32, jnp.int32
    vmem = pltpu.VMEM
    totals = pl.pallas_call(
        functools.partial(kernel, n_pages, n_blocks, qtok),
        out_shape=vmem((owned, n_pages, slots), f32),
        in_specs=[pl.BlockSpec(memory_space=pl.ANY)] * len(args),
        out_specs=pl.BlockSpec(memory_space=pltpu.VMEM),
        scratch_shapes=[
            vmem((cents, width), bf16),
            vmem((cents, rank, width), bf16),
            vmem((pages, patches), i32),
            pltpu.SMEM((pages, patches), i32),
            vmem((pages, patches * rank), bf16),
            vmem((2, 1, pages), i32),
            vmem((2, slots, n_query), i32),
            vmem((2, 1, n_query), i32),
            vmem((n_blocks * nz * rows_q, width), bf16),
            vmem((DEPTH // rank, pages, width), f32),
            vmem((2, patches * pages, width), bf16),
            vmem((pages, width), f32),
            vmem((2, pages, width), f32),
            vmem((2 * n_blocks, 2 * pages, pad), bf16),
            vmem((2 * n_blocks, 2 * pages, pad), bf16),
            vmem((-(-n_query // 128) * 128, width), f32),
            vmem((nz, owned, width), f32),
            vmem((nz, owned, width), f32),
            dma((9,)),
            dma, dma((2,)),
            dma, dma,
            dma((3,)), dma((3,)),
            dma, dma((2,)),
            dma, dma,
        ],
        compiler_params=pltpu.CompilerParams(collective_id=0, has_side_effects=True),
    )(*args)
    return totals / qtok


def solution(mesh):
    placed = (
        P(("pages", "blocks"), None, None),
        P(),
        P(),
        P("pages", None, "blocks"),
        P("pages", None, "blocks"),
        P("pages", None),
        P("pages", None, None),
        P("pages", None),
    )
    return jax.shard_map(
        on_device,
        mesh=mesh,
        in_specs=placed,
        out_specs=P(("pages", "blocks"), None, None),
        check_vma=False,
    )
```
